128 devices in a mesh: sec: 16 (over y, x_hi, core), lane: 8 (over z, x_lo).
Axes of the slice: x: 4 (x_hi: 2, x_lo: 2; x = x_hi * 2 + x_lo), y: 4, z: 4, core: 2. Of those that a mesh axis runs over, the one named last changes fastest.
Arguments:
- queries: bfloat16 [16, 384, 5120], P('sec', None, 'lane'), may hold values from -40 to 40
- key_value: bfloat16 [4096, 2, 1024], P('sec', None, 'lane'), may hold values from -6 to 6
- grad_out: bfloat16 [16, 384, 5120], P('sec', None, 'lane'), may hold values from -12 to 12
- inputs: bfloat16 [4096, 5120], P('sec'), may hold values from -6 to 6
- w_kv: bfloat16 [5120, 2, 1024], P('sec'), may hold values from -0.078125 to 0.078125
Outputs:
- grad_queries: bfloat16 [16, 384, 5120], P('sec', None, 'lane')
- grad_inputs: bfloat16 [4096, 5120], P(('sec', 'lane'))
- grad_w_kv: float32 [5120, 2, 1024], P('sec', None, 'lane')
The draws below stay inside these ranges and needn't reach their ends.
All inputs are finite; a program needn't handle non-finite values.
Results may differ from the reference program's by a relative error of at most 0.0058.
Values may be sent and summed in bfloat16 or wider, within the bound.
A program may use at most 128 MiB of HBM per device.

```python
import math
import jax
import jax.numpy as jnp
from jax import lax

D = 5120
NQH = 40
KVH = 8
HD = 128
QLEN = 384
SECS = 16
POS = 4096


def joint_draw(key):
    base = jax.random.fold_in(key, 101)
    keys = jnp.clip(jax.random.normal(jax.random.fold_in(base, 1), (POS, KVH, HD), jnp.float32), -4.0, 4.0)
    queries = jnp.clip(1.5 * jax.random.normal(jax.random.fold_in(base, 2), (SECS, QLEN, NQH, HD), jnp.float32), -6.0, 6.0)
    values = jnp.clip(jax.random.normal(jax.random.fold_in(base, 3), (POS, KVH, HD), jnp.float32), -6.0, 6.0)
    stacked = jnp.stack([keys.reshape(POS, KVH * HD), values.reshape(POS, KVH * HD)], axis=1)
    return (queries.reshape(SECS, QLEN, NQH * HD), stacked)


def draw_queries(key, part):
    return joint_draw(key)[0].astype(jnp.bfloat16)


def draw_key_value(key, part):
    return joint_draw(key)[1].astype(jnp.bfloat16)


def block_scale(key, dims, cuts, least, largest):
    loudness, own = 1.0, jax.random.fold_in(key, 6)
    for axis_at, blocks in cuts:
        steps = jnp.exp(jax.random.uniform(jax.random.fold_in(own, axis_at), (blocks,), jnp.float32, least / len(cuts), largest / len(cuts)))
        loudness = loudness * jnp.repeat(steps, dims[axis_at] // blocks).reshape([-1 if axis == axis_at else 1 for axis in range(len(dims))])
    return loudness


def scatter_about(key, shape, deviation, reach, shards=(), kind=jnp.bfloat16):
    entries = jax.random.normal(key, shape, jnp.float32) * deviation
    if len(shards) > 0:
        entries = block_scale(key, shape, shards, -0.22, 0.18) * entries
    return jnp.clip(entries, min=-reach, max=reach).astype(kind)


def setup_inputs(seed: int = 0) -> dict:
    seeds = jax.random.split(jax.random.key(seed), 6)
    return {
        "queries": draw_queries(jax.random.fold_in(seeds[5], 71), 0),
        "key_value": draw_key_value(jax.random.fold_in(seeds[5], 71), 0),
        "grad_out": scatter_about(seeds[2], (SECS, QLEN, NQH * HD), 2.0, 12.0, ((0, 16), (2, 8))),
        "inputs": scatter_about(seeds[3], (POS, D), 1.0, 6.0, ((0, 16),)),
        "w_kv": scatter_about(seeds[4], (D, 2, KVH * HD), D ** -0.5, 0.078125, ((0, 16),)),
    }


def row_stats(raw, dprobs, block_count):
    rows = raw.shape[0]
    width = raw.shape[1] // block_count
    raw_blocks = raw.reshape(rows, block_count, width).transpose(1, 0, 2)
    dp_blocks = dprobs.reshape(rows, block_count, width).transpose(1, 0, 2)

    def step(carry, items):
        run_max, run_sum, run_dot = carry
        masked, dp_block = items
        new_max = jnp.maximum(run_max, jnp.max(masked, axis=1))
        factor = jnp.exp(run_max - new_max)
        weights = jnp.exp(masked - new_max[:, None])
        run_sum = run_sum * factor + jnp.sum(weights, axis=1)
        run_dot = run_dot * factor + jnp.sum(weights * dp_block, axis=1)
        return (new_max, run_sum, run_dot), None

    start_max = jnp.full((rows,), -1e30, jnp.float32)
    start_zero = jnp.zeros((rows,), jnp.float32)
    (run_max, run_sum, run_dot), _ = lax.scan(step, (start_max, start_zero, start_zero), (raw_blocks, dp_blocks))
    return run_max + jnp.log(run_sum), run_dot / run_sum


def reference(queries, key_value, grad_out, inputs, w_kv):
    group_size = NQH // KVH
    softmax_scale = HD ** -0.5
    keys = key_value[:, 0]
    values = key_value[:, 1]
    block_count = math.gcd(POS, max(1, POS // 512))
    last_key = POS - QLEN + jnp.arange(QLEN * group_size) // group_size
    visible = jnp.arange(POS)[None, :] <= last_key[:, None]

    def section(carry, items):
        query_sec, grad_sec = items
        dq_list = []
        dk_list = []
        dv_list = []
        for kv_head in range(KVH):
            q_rows = query_sec[:, kv_head * group_size * HD:(kv_head + 1) * group_size * HD].reshape(QLEN * group_size, HD)
            do_rows = grad_sec[:, kv_head * group_size * HD:(kv_head + 1) * group_size * HD].reshape(QLEN * group_size, HD)
            k_head = keys[:, kv_head * HD:(kv_head + 1) * HD]
            v_head = values[:, kv_head * HD:(kv_head + 1) * HD]
            raw = jnp.dot(q_rows, k_head.T, preferred_element_type=jnp.float32) * softmax_scale
            raw = jnp.where(visible, raw, -jnp.inf)
            dprobs = jnp.dot(do_rows, v_head.T, preferred_element_type=jnp.float32)
            lse, row_delta = row_stats(raw, dprobs, block_count)
            probs = jnp.where(visible, jnp.exp(raw - lse[:, None]), 0.0)
            dscores = (probs * (dprobs - row_delta[:, None])).astype(jnp.bfloat16)
            probs_low = probs.astype(jnp.bfloat16)
            dq_head = jnp.dot(dscores, k_head, preferred_element_type=jnp.float32) * softmax_scale
            dq_list.append(dq_head.reshape(QLEN, group_size * HD))
            dk_list.append(jnp.dot(dscores.T, q_rows, preferred_element_type=jnp.float32) * softmax_scale)
            dv_list.append(jnp.dot(probs_low.T, do_rows, preferred_element_type=jnp.float32))
        part = jnp.stack([jnp.concatenate(dk_list, axis=1), jnp.concatenate(dv_list, axis=1)], axis=1)
        return carry + part, jnp.concatenate(dq_list, axis=1).astype(jnp.bfloat16)

    start_sum = jnp.zeros((POS, 2, KVH * HD), jnp.float32)
    total, grad_queries = lax.scan(section, start_sum, (queries, grad_out))
    dkv = total.astype(jnp.bfloat16)
    flat_grads = dkv.reshape(POS, 2 * KVH * HD)
    flat_weights = w_kv.reshape(D, 2 * KVH * HD)
    grad_inputs = jnp.dot(flat_grads, flat_weights.T, preferred_element_type=jnp.float32).astype(jnp.bfloat16)
    grad_w_kv = jnp.dot(inputs.T, flat_grads, preferred_element_type=jnp.float32).reshape(D, 2, KVH * HD)
    return grad_queries, grad_inputs, grad_w_kv
```

```python
import functools

import jax
import jax.numpy as jnp
from jax import lax
from jax.experimental import pallas as pl
from jax.experimental.pallas import tpu as pltpu
from jax.sharding import PartitionSpec as P

HD = 128
SCALE = HD**-0.5
SCALE_LOG2E = SCALE * 1.4426950408889634
MESH = pl.DeviceIdType.MESH
f32, bf16 = jnp.float32, jnp.bfloat16
NT = (((1,), (1,)), ((), ()))
TN = (((0,), (0,)), ((), ()))
NN = (((1,), (0,)), ((), ()))
dot = functools.partial(lax.dot_general, preferred_element_type=f32)

CHIPS = 8
LANES = 8
ROWS = 256
KEYS = 4096
QL = 384
GROUP = 5
BLK = 256
NBLK = 8
CH = 2048
SUB = 64
DCOL = 640


def kernel(
    q_ref, do_ref, kv_ref, x_ref, w_ref, dq_ref, gi_ref, gw_ref,
    kvall, qs, dos, kT, ebuf, dpbuf, mbuf, acc, psend, precv, rsend, rrecv,
    dall, gin, xall, wall, gsend, gout, term, trecv,
    loc, kv_s, kv_r, kvf_s, kvf_r, x1_s, x1_r, x2_s, x2_r, w_s, w_r,
    p_s, p_r, r_s, r_r, a_s, a_r, g_s, g_r, o_s, o_r, t_s, t_r,
):
    s = lax.axis_index("sec")
    lane = lax.axis_index("lane")
    core = s % 2
    chip = s // 2
    partner = {"sec": chip * 2 + 1 - core, "lane": lane}

    def at_chip(k):
        return {"sec": k * 2 + core, "lane": lane}

    def at_lane(t):
        return {"sec": s, "lane": t}

    def remote(src, dst, ssem, rsem, to):
        return pltpu.make_async_remote_copy(
            src_ref=src, dst_ref=dst, send_sem=ssem, recv_sem=rsem, device_id=to, device_id_type=MESH
        )

    barrier = pltpu.get_barrier_semaphore()
    pl.semaphore_signal(barrier, inc=1, device_id=partner, device_id_type=MESH)
    for d in range(1, 8):
        pl.semaphore_signal(barrier, inc=1, device_id=at_chip((chip + d) % 8), device_id_type=MESH)
        pl.semaphore_signal(barrier, inc=1, device_id=at_lane((lane + d) % 8), device_id_type=MESH)

    local = [
        pltpu.make_async_copy(kv_ref, kvall.at[pl.ds(s * ROWS, ROWS)], loc.at[0]),
        pltpu.make_async_copy(
            x_ref.at[pl.ds(lane * 32, 32), pl.ds(chip * DCOL, DCOL)],
            xall.at[chip, pl.ds(lane * 32, 32)],
            loc.at[1],
        ),
        pltpu.make_async_copy(w_ref, wall.at[pl.ds(core * 320, 320)], loc.at[2]),
    ]
    for copy in local:
        copy.start()
    for h in range(GROUP):
        qs[h * QL : (h + 1) * QL, :] = q_ref[:, h * HD : (h + 1) * HD]
        dos[h * QL : (h + 1) * QL, :] = do_ref[:, h * HD : (h + 1) * HD]
    qs[GROUP * QL :, :] = jnp.zeros((NBLK * BLK - GROUP * QL, HD), bf16)
    dos[GROUP * QL :, :] = jnp.zeros((NBLK * BLK - GROUP * QL, HD), bf16)
    pl.semaphore_wait(barrier, 15)

    mine = kvall.at[pl.ds(s * ROWS, ROWS)]
    kv_out = [
        remote(kv_ref, mine, kv_s.at[d - 1], kv_r.at[d - 1], at_chip((chip + d) % 8)) for d in range(1, 8)
    ]
    kv_fwd = [remote(kv_ref, mine, kvf_s.at[0], kvf_r.at[0], partner)]
    for copy in kv_out + kv_fwd:
        copy.start()
    x_out = [
        remote(
            x_ref.at[pl.ds(lane * 32, 32), pl.ds(((chip + d) % 8) * DCOL, DCOL)],
            xall.at[chip, pl.ds(lane * 32, 32)],
            x1_s.at[d - 1],
            x1_r.at[d - 1],
            at_chip((chip + d) % 8),
        )
        for d in range(1, 8)
    ]
    w_out = remote(w_ref, wall.at[pl.ds(core * 320, 320)], w_s, w_r, partner)
    for copy in x_out:
        copy.start()
    w_out.start()
    for d in range(1, 8):
        kv_out[d - 1].wait_recv()
        part = kvall.at[pl.ds((((chip + 8 - d) % 8) * 2 + core) * ROWS, ROWS)]
        copy = remote(part, part, kvf_s.at[d], kvf_r.at[d], partner)
        copy.start()
        kv_fwd.append(copy)
    local[0].wait()
    local[1].wait()
    for copy in x_out:
        copy.wait_recv()
    rows_here = xall.at[:, pl.ds(lane * 32, 32)]
    x_lane = [
        remote(rows_here, rows_here, x2_s.at[d - 1], x2_r.at[d - 1], at_lane((lane + d) % 8))
        for d in range(1, 8)
    ]
    for copy in x_lane:
        copy.start()
    for copy in kv_fwd:
        copy.wait_recv()

    kT[...] = kvall[:, 0:HD].T

    def block(b, first):
        rows = pl.ds(b * BLK, BLK)
        qb = qs[rows, :]
        dob = dos[rows, :]
        i0 = (b * BLK) % QL

        def stage_a(ch, carry, mask):
            base = ch * CH
            scores = dot(kvall[pl.ds(base, CH), 0:HD], qb, NT)
            dprobs = dot(kvall[pl.ds(base, CH), HD : 2 * HD], dob, NT)
            m, total, dots = carry
            for u in range(CH // SUB):
                sc = scores[u * SUB : (u + 1) * SUB]
                dp = dprobs[u * SUB : (u + 1) * SUB]
                if mask and base + (u + 1) * SUB > KEYS - QL:
                    j = lax.broadcasted_iota(jnp.int32, (SUB, BLK), 0) + (base + u * SUB - (KEYS - QL))
                    i = lax.broadcasted_iota(jnp.int32, (SUB, BLK), 1) + i0
                    i = jnp.where(i >= QL, i - QL, i)
                    sc = jnp.where(j <= i, sc, -1e30)
                sc = sc.reshape(SUB // 8, 8, BLK)
                dp8 = dp.reshape(SUB // 8, 8, BLK)
                top = jnp.max(sc, axis=0) * SCALE_LOG2E
                e = jnp.exp2(sc * SCALE_LOG2E - top[None])
                part = jnp.sum(e, axis=0)
                part_dot = jnp.sum(e * dp8, axis=0)
                ebuf[pl.ds(base + u * SUB, SUB), :] = e.reshape(SUB, BLK)
                dpbuf[pl.ds(base + u * SUB, SUB), :] = dp
                mbuf[ch * (CH // SUB) + u] = top
                new = jnp.maximum(m, top)
                old_f = jnp.exp2(m - new)
                new_f = jnp.exp2(top - new)
                total = total * old_f + part * new_f
                dots = dots * old_f + part_dot * new_f
                m = new
            return m, total, dots

        zero = jnp.zeros((8, BLK), f32)
        carry = (jnp.full((8, BLK), -1e35, f32), zero, zero)
        for ch in range(KEYS // CH):
            carry = stage_a(ch, carry, ch == KEYS // CH - 1)
        m, total, dots = carry
        top = jnp.max(m, axis=0, keepdims=True)
        f = jnp.exp2(m - top)
        inv = 1.0 / jnp.sum(total * f, axis=0, keepdims=True)
        delta = jnp.sum(dots * f, axis=0, keepdims=True) * inv
        delta8 = jnp.broadcast_to(delta, (8, BLK))
        inv8 = jnp.broadcast_to(inv, (8, BLK))
        top8 = jnp.broadcast_to(top, (8, BLK))

        def stage_c(ch, dq):
            base = ch * CH
            probs, dscores = [], []
            for u in range(CH // SUB):
                f = jnp.exp2(mbuf[ch * (CH // SUB) + u] - top8) * inv8
                e = ebuf[pl.ds(base + u * SUB, SUB), :].reshape(SUB // 8, 8, BLK)
                dp = dpbuf[pl.ds(base + u * SUB, SUB), :].reshape(SUB // 8, 8, BLK)
                p = e * f[None]
                probs.append(p.reshape(SUB, BLK).astype(bf16))
                dscores.append((p * (dp - delta8[None])).reshape(SUB, BLK).astype(bf16))
            probs = jnp.concatenate(probs, axis=0)
            dscores = jnp.concatenate(dscores, axis=0)
            dv = dot(probs, dob, NN)
            dk = dot(dscores, qb, NN)
            if first:
                acc[pl.ds(base, CH), 0:HD] = dk
                acc[pl.ds(base, CH), HD : 2 * HD] = dv
            else:
                acc[pl.ds(base, CH), 0:HD] += dk
                acc[pl.ds(base, CH), HD : 2 * HD] += dv
            return dq + dot(kT[:, pl.ds(base, CH)], dscores, NN)

        dq = lax.fori_loop(0, KEYS // CH, stage_c, jnp.zeros((HD, BLK), f32))
        qs[rows, :] = (dq.T * SCALE).astype(bf16)

    block(0, True)

    def body(b, carry):
        block(b, False)
        return carry

    lax.fori_loop(1, NBLK, body, 0)
    for h in range(GROUP):
        dq_ref[:, h * HD : (h + 1) * HD] = qs[h * QL : (h + 1) * QL, :]

    def pair(rows):
        part = acc[rows, :]
        col = lax.broadcasted_iota(jnp.int32, (ROWS, 2 * HD), 1)
        return jnp.where(col < HD, part * SCALE, part)

    p_out = []
    for d in range(1, 9):
        k = (chip + d) % 8
        psend[d - 1] = pair(pl.ds((2 * k + 1 - core) * ROWS, ROWS)).astype(bf16)
        copy = remote(psend.at[d - 1], precv.at[d - 1], p_s.at[d - 1], p_r.at[d - 1], partner)
        copy.start()
        p_out.append(copy)
    r_out = []
    own = None
    for d in range(1, 9):
        k = (chip + d) % 8
        part = pair(pl.ds((2 * k + core) * ROWS, ROWS))
        p_out[d - 1].wait_recv()
        both = part + precv[d - 1].astype(f32)
        if d < 8:
            rsend[d - 1] = both.astype(bf16)
            copy = remote(rsend.at[d - 1], rrecv.at[d - 1], r_s.at[d - 1], r_r.at[d - 1], at_chip(k))
            copy.start()
            r_out.append(copy)
        else:
            own = both
    for d in range(1, 8):
        r_out[d - 1].wait_recv()
        own = own + rrecv[d - 1].astype(f32)
    dall[chip] = own.astype(bf16)

    a_out = [
        remote(dall.at[chip], dall.at[chip], a_s.at[d - 1], a_r.at[d - 1], at_chip((chip + d) % 8))
        for d in range(1, 8)
    ]
    for copy in a_out:
        copy.start()

    def to_lane(k):
        return remote(dall.at[k], gin.at[lane], g_s.at[k], g_r.at[lane], at_lane(k))

    def stay(k):
        return pltpu.make_async_copy(dall.at[k], gin.at[lane], g_r.at[lane])

    def pass_on(k):
        @pl.when(k != lane)
        def _():
            to_lane(k).start()

        @pl.when(k == lane)
        def _():
            stay(k).start()

    pass_on(chip)
    local[2].wait()
    w_out.wait()
    for copy in x_lane:
        copy.wait()
    for d in range(1, 8):
        a_out[d - 1].wait_recv()
        pass_on((chip + 8 - d) % 8)

    total = dot(xall[0], dall[0], TN)
    for k in range(1, 8):
        total = total + dot(xall[k], dall[k], TN)
    term[...] = total
    t_out = remote(term.at[pl.ds((1 - core) * 320, 320)], trecv, t_s, t_r, partner)
    t_out.start()

    for t in range(8):

        @pl.when(t != lane)
        def _():
            remote(dall.at[t], gin.at[t], g_s.at[t], g_r.at[t], at_lane(t)).wait_recv()

        @pl.when(t == lane)
        def _():
            stay(t).wait()

    grads = dot(gin[0], wall[:, 0 : 2 * HD], NT)
    for t in range(1, 8):
        grads = grads + dot(gin[t], wall[:, t * 2 * HD : (t + 1) * 2 * HD], NT)
    gsend[...] = grads.astype(bf16)

    cols = pl.ds(chip * DCOL, DCOL)

    def hand(t):
        return remote(
            gsend.at[pl.ds(t * 32, 32)],
            gout.at[:, cols],
            o_s.at[t],
            o_r.at[chip],
            {"sec": lane * 2 + core, "lane": t},
        )

    def hand_here(t):
        return pltpu.make_async_copy(gsend.at[pl.ds(t * 32, 32)], gout.at[:, cols], o_r.at[chip])

    for t in range(8):
        here = jnp.logical_and(lane == chip, lane == t)

        @pl.when(jnp.logical_not(here))
        def _():
            hand(t).start()

        @pl.when(here)
        def _():
            hand_here(t).start()

    t_out.wait_recv()
    gw_ref[...] = term[pl.ds(core * 320, 320), :] + trecv[...]

    for k in range(8):
        here = jnp.logical_and(lane == chip, k == chip)
        arrived = gout.at[:, pl.ds(k * DCOL, DCOL)]

        @pl.when(jnp.logical_not(here))
        def _():
            remote(
                gsend.at[pl.ds(0, 32)], arrived, o_s.at[k], o_r.at[k], {"sec": k * 2 + core, "lane": chip}
            ).wait_recv()

        @pl.when(here)
        def _():
            pltpu.make_async_copy(gsend.at[pl.ds(0, 32)], arrived, o_r.at[k]).wait()

    gi_ref[...] = gout[...]

    for copy in kv_out + kv_fwd + x_out + p_out + r_out + a_out + [t_out]:
        copy.wait_send()
    for t in range(8):

        @pl.when(t != lane)
        def _():
            remote(dall.at[t], gin.at[lane], g_s.at[t], g_r.at[lane], at_lane(t)).wait_send()

        @pl.when(jnp.logical_not(jnp.logical_and(lane == chip, lane == t)))
        def _():
            hand(t).wait_send()


def local_step(queries, key_value, grad_out, inputs, w_kv):
    kv = key_value.reshape(ROWS, 2 * HD)
    w = w_kv.reshape(320, 2, LANES, HD).transpose(0, 2, 1, 3).reshape(320, 2 * LANES * HD)
    vmem = pltpu.VMEM
    dma = pltpu.SemaphoreType.DMA
    whole = pl.BlockSpec(memory_space=vmem)
    there = pl.BlockSpec(memory_space=pl.ANY)
    blocks = (CHIPS, ROWS, 2 * HD)
    grad_queries, grad_inputs, grad_w = pl.pallas_call(
        kernel,
        out_shape=(
            jax.ShapeDtypeStruct((QL, GROUP * HD), bf16),
            jax.ShapeDtypeStruct((32, CHIPS * DCOL), bf16),
            jax.ShapeDtypeStruct((320, 2 * HD), f32),
        ),
        in_specs=[whole, whole, whole, there, there],
        out_specs=(whole, whole, whole),
        scratch_shapes=[
            vmem((KEYS, 2 * HD), bf16),
            vmem((NBLK * BLK, HD), bf16),
            vmem((NBLK * BLK, HD), bf16),
            vmem((HD, KEYS), bf16),
            vmem((KEYS, BLK), f32),
            vmem((KEYS, BLK), f32),
            vmem((KEYS // SUB, 8, BLK), f32),
            vmem((KEYS, 2 * HD), f32),
            vmem(blocks, bf16),
            vmem(blocks, bf16),
            vmem((7, ROWS, 2 * HD), bf16),
            vmem((7, ROWS, 2 * HD), bf16),
            vmem(blocks, bf16),
            vmem(blocks, bf16),
            vmem((CHIPS, ROWS, DCOL), bf16),
            vmem((DCOL, 2 * LANES * HD), bf16),
            vmem((ROWS, DCOL), bf16),
            vmem((32, CHIPS * DCOL), bf16),
            vmem((DCOL, 2 * HD), f32),
            vmem((320, 2 * HD), f32),
            dma((3,)),
            dma((7,)), dma((7,)), dma((8,)), dma((8,)), dma((7,)), dma((7,)), dma((7,)), dma((7,)), dma, dma,
            dma((8,)), dma((8,)), dma((7,)), dma((7,)), dma((7,)), dma((7,)), dma((8,)), dma((8,)),
            dma((8,)), dma((8,)), dma, dma,
        ],
        compiler_params=pltpu.CompilerParams(
            collective_id=0, has_side_effects=True, vmem_limit_bytes=60 * 2**20
        ),
        name="step",
    )(queries[0], grad_out[0], kv, inputs, w)
    return grad_queries[None], grad_inputs, grad_w.reshape(320, 2, HD)


def solution(mesh):
    in_specs = (
        P("sec", None, "lane"),
        P("sec", None, "lane"),
        P("sec", None, "lane"),
        P("sec", None),
        P("sec", None, None),
    )
    out_specs = (P("sec", None, "lane"), P(("sec", "lane"), None), P("sec", None, "lane"))
    return jax.shard_map(local_step, mesh=mesh, in_specs=in_specs, out_specs=out_specs, check_vma=False)
```
